32 devices in a mesh: illum: 2 (over y), gx: 4 (over x, core), gy: 4 (over z).
Axes of the slice: x: 2, y: 2, z: 4, core: 2. Of those that a mesh axis runs over, the one named last changes fastest.
Arguments:
- density: float32 [128, 64, 128], P('gx', 'gy'), may hold values from 0 to 1
- moment_one: float32 [128, 64, 128], P('gx', 'gy'), may hold values from -0.6 to 0.6
- moment_two: float32 [128, 64, 128], P('gx', 'gy'), may hold values from 0.0002 to 0.0006
- forward_field: bfloat16 [2, 2, 3, 128, 64, 128], P('illum', None, None, 'gx', 'gy'), may hold values from -6 to 6
- adjoint_field: bfloat16 [2, 2, 3, 128, 64, 128], P('illum', None, None, 'gx', 'gy'), may hold values from -6 to 6
- objective_weight: float32 [2], P('illum'), may hold values from 0.02 to 0.2
Outputs:
- new_density: float32 [128, 64, 128], P('gx', 'gy')
- new_moment_one: float32 [128, 64, 128], P('gx', 'gy')
- new_moment_two: float32 [128, 64, 128], P('gx', 'gy')
- physical: float32 [128, 64, 128], P('gx', 'gy')
The draws below stay inside these ranges and needn't reach their ends.
All inputs are finite; a program needn't handle non-finite values.
Results may differ from the reference program's by a relative error of at most 0.0003.
Values sent between devices are 32-bit elements; how exact they have to be, the bound alone decides.
A program may use at most 64 MiB of HBM per device.

```python
import math
import jax
import jax.numpy as jnp
from jax import lax

RADIUS = 8
SOURCES = 2
NX = 128
NY = 64
NZ = 128


def level_of(stream_key, shape, cuts, smallest, largest):
    gain, own = 1.0, jax.random.fold_in(stream_key, 6)
    for dim, shards_of in cuts:
        heights = jnp.exp(jax.random.uniform(jax.random.fold_in(own, dim), (shards_of,), jnp.float32, smallest / len(cuts), largest / len(cuts)))
        gain = gain * jnp.repeat(heights, shape[dim] // shards_of).reshape([-1 if axis == dim else 1 for axis in range(len(shape))])
    return gain


def normal_values(own_key, dims, width, most, split=(), kind=jnp.bfloat16):
    array = width * jax.random.normal(own_key, dims, jnp.float32)
    if split:
        array = array * level_of(own_key, dims, split, -0.22, 0.18)
    return jnp.clip(array, -most, most).astype(kind)


def setup_inputs(seed: int = 0) -> dict:
    key_list = jax.random.split(jax.random.key(seed), 7)
    return {
        "density": jnp.clip(1.0 * jax.random.uniform(key_list[0], (NX, NY, NZ), jnp.float32) ** level_of(key_list[0], (NX, NY, NZ), ((0, 4), (1, 4)), -0.2, 0.2), 0.0, 1.0),
        "moment_one": jnp.clip(jax.random.uniform(key_list[1], (NX, NY, NZ), jnp.float32, -0.6, 0.6) * level_of(key_list[1], (NX, NY, NZ), ((0, 4), (1, 4)), -0.4, 0.0), -0.6, 0.6),
        "moment_two": jnp.clip(jnp.exp(math.log(0.0006) - 1.09861236 * jax.random.uniform(key_list[2], (NX, NY, NZ), jnp.float32) ** level_of(key_list[2], (NX, NY, NZ), ((0, 4), (1, 4)), -0.2, 0.2)), 0.0002, 0.0006),
        "forward_field": normal_values(key_list[3], (SOURCES, 2, 3, NX, NY, NZ), 1.0, 6.0, ((0, 2), (3, 4), (4, 4))),
        "adjoint_field": normal_values(key_list[4], (SOURCES, 2, 3, NX, NY, NZ), 1.0, 6.0, ((0, 2), (3, 4), (4, 4))),
        "objective_weight": jnp.clip(jnp.exp(math.log(0.2) - 2.3025851 * jax.random.uniform(key_list[5], (SOURCES,), jnp.float32) ** level_of(key_list[5], (SOURCES,), ((0, 2),), -0.2, 0.2)), 0.02, 0.2),
    }


sharpness = 8.0
threshold = 0.5

def tap_weights():
    offsets = jnp.arange(-RADIUS, RADIUS + 1)
    return ((RADIUS + 1 - jnp.abs(offsets)) / (RADIUS + 1) ** 2).astype(jnp.float32)

def band_matrix(length):
    rows = jnp.arange(length)[:, None]
    cols = jnp.arange(length)[None, :]
    apart = jnp.abs(rows - cols)
    values = (RADIUS + 1 - apart).astype(jnp.float32) / float((RADIUS + 1) ** 2)
    return jnp.where(apart <= RADIUS, values, jnp.float32(0.0))

def line_filter(padded, axis, length):
    weights = tap_weights()
    total = jnp.zeros(padded.shape[:axis] + (length,) + padded.shape[axis + 1:], jnp.float32)
    for offset in range(2 * RADIUS + 1):
        total = total + weights[offset] * lax.slice_in_dim(padded, offset, offset + length, axis=axis)
    return total

def depth_filter(field):
    shape = field.shape
    flat = field.reshape(-1, shape[2])
    out = jnp.dot(flat, band_matrix(shape[2]), precision=lax.Precision.HIGHEST, preferred_element_type=jnp.float32)
    return out.reshape(shape)

def full_filter(field):
    padded = jnp.pad(field, ((RADIUS, RADIUS), (RADIUS, RADIUS), (0, 0)))
    along_x = line_filter(padded, 0, field.shape[0])
    along_y = line_filter(along_x, 1, field.shape[1])
    return depth_filter(along_y)

def project(value):
    scale = jnp.tanh(sharpness * threshold) + jnp.tanh(sharpness * (1.0 - threshold))
    return (jnp.tanh(sharpness * threshold) + jnp.tanh(sharpness * (value - threshold))) / scale

def slope(value):
    scale = jnp.tanh(sharpness * threshold) + jnp.tanh(sharpness * (1.0 - threshold))
    inner = jnp.tanh(sharpness * (value - threshold))
    return sharpness * (1.0 - inner * inner) / scale

def reference(density, moment_one, moment_two, forward_field, adjoint_field, objective_weight):
    filtered = full_filter(density)

    def one_source(items):
        fwd, adj, weight = items
        fwd = fwd.astype(jnp.float32)
        adj = adj.astype(jnp.float32)
        intersection = lax.optimization_barrier(jnp.sum(fwd[0] * adj[0] - fwd[1] * adj[1], axis=0))
        return weight * intersection
    terms = lax.map(one_source, (forward_field, adjoint_field, objective_weight))
    sensitivity = lax.optimization_barrier(jnp.sum(terms, axis=0))
    chained = sensitivity * slope(filtered)
    gradient = full_filter(chained)
    new_moment_one = 0.9 * moment_one + 0.1 * gradient
    new_moment_two = 0.999 * moment_two + 0.001 * gradient * gradient
    first_fix = 1.0 - 0.9 ** 5
    second_fix = 1.0 - 0.999 ** 5
    step = new_moment_one / first_fix / (jnp.sqrt(new_moment_two / second_fix) + 1e-08)
    new_density = jnp.clip(density - 0.05 * step, 0.0, 1.0)
    physical = project(full_filter(new_density))
    return (new_density, new_moment_one, new_moment_two, physical)
```

```python
import functools
import math

import jax
import jax.numpy as jnp
from jax import lax
from jax.experimental import pallas as pl
from jax.experimental.pallas import tpu as pltpu
from jax.sharding import PartitionSpec as P

RADIUS = 8
SHARPNESS = 8.0
THRESHOLD = 0.5
TANH_EDGE = math.tanh(SHARPNESS * THRESHOLD)
SCALE = math.tanh(SHARPNESS * THRESHOLD) + math.tanh(SHARPNESS * (1.0 - THRESHOLD))
NORM = 1.0 / float((RADIUS + 1) ** 6)
FIRST_FIX = 1.0 / (1.0 - 0.9**5)
SECOND_FIX = 1.0 / (1.0 - 0.999**5)
MESH = pl.DeviceIdType.MESH
ROUNDS = 3


def split(value):
    high = value.astype(jnp.bfloat16)
    low = (value - high.astype(jnp.float32)).astype(jnp.bfloat16)
    return high, low


def box(value):
    n = value.shape[0]
    two = value[: n - 1] + value[1:]
    four = two[: n - 3] + two[2:]
    eight = four[: n - 7] + four[4:]
    return eight[: n - 8] + value[8:]


def plane_matrix(tile_y, group):
    rows, cols = group * tile_y, group * (tile_y + 2 * RADIUS)
    row = lax.broadcasted_iota(jnp.int32, (rows, cols), 0)
    col = lax.broadcasted_iota(jnp.int32, (rows, cols), 1)
    padded = tile_y + 2 * RADIUS
    plane = row // tile_y
    apart = jnp.abs((col - plane * padded) - (row - plane * tile_y) - RADIUS)
    taps = jnp.maximum(RADIUS + 1 - apart, 0)
    return taps.astype(jnp.float32).astype(jnp.bfloat16)


def depth_matrix(length):
    row = lax.broadcasted_iota(jnp.int32, (2 * length, length), 0)
    col = lax.broadcasted_iota(jnp.int32, (2 * length, length), 1)
    row = jnp.where(row >= length, row - length, row)
    taps = jnp.maximum(RADIUS + 1 - jnp.abs(row - col), 0)
    return taps.astype(jnp.float32).astype(jnp.bfloat16)


def kernel(
    sizes,
    den,
    m1,
    m2,
    fwd,
    adj,
    weight,
    new_den,
    new_m1,
    new_m2,
    physical,
    ybuf,
    xbuf,
    sens,
    fbuf,
    abuf,
    m1buf,
    m2buf,
    dbuf,
    pbuf,
    filt,
    local_sem,
    out_sem,
    y_send,
    y_recv,
    x_send,
    x_recv,
    s_send,
    s_recv,
):
    n_illum, n_gx, n_gy = sizes
    tile_x, tile_y, depth = den.shape
    sources, _, comps = fwd.shape[:3]
    me = lax.axis_index("illum")
    gx = lax.axis_index("gx")
    gy = lax.axis_index("gy")
    pieces = [(0, RADIUS), (tile_x - RADIUS, RADIUS), (RADIUS, tile_x - 2 * RADIUS)]
    own = pl.ds(RADIUS, tile_y)

    loads = {}

    def load(name, src, dst):
        copy = pltpu.make_async_copy(src, dst, local_sem.at[len(loads)])
        copy.start()
        loads[name] = copy

    for i, (p, n) in enumerate(pieces):
        part = pl.ds(p, n)
        load(("f", i), fwd.at[:, :, :, part], fbuf.at[:, :, :, part])
        load(("a", i), adj.at[:, :, :, part], abuf.at[:, :, :, part])
    load("d", den, ybuf.at[0, :, own])
    load("m1", m1, m1buf)
    load("m2", m2, m2buf)

    x_prev = (gx > 0, {"gx": jnp.maximum(gx - 1, 0)})
    x_next = (gx < n_gx - 1, {"gx": jnp.minimum(gx + 1, n_gx - 1)})
    y_prev = (gy > 0, {"gy": jnp.maximum(gy - 1, 0)})
    y_next = (gy < n_gy - 1, {"gy": jnp.minimum(gy + 1, n_gy - 1)})
    others = [{"illum": lax.rem(me + k, n_illum)} for k in range(1, n_illum)]

    barrier = pltpu.get_barrier_semaphore()
    for there, device in (y_prev, y_next, x_prev, x_next):

        @pl.when(there)
        def _(device=device):
            pl.semaphore_signal(barrier, inc=1, device_id=device, device_id_type=MESH)

    for device in others:
        pl.semaphore_signal(barrier, inc=1, device_id=device, device_id_type=MESH)
    peers = jnp.int32(len(others))
    for there, _ in (y_prev, y_next, x_prev, x_next):
        peers = peers + there.astype(jnp.int32)
    pl.semaphore_wait(barrier, peers)

    def y_copy(r, d, i, source=None):
        p, n = pieces[i]
        part = pl.ds(p, n)
        if d == 0:
            rows, land, device = RADIUS, RADIUS + tile_y, y_prev[1]
        else:
            rows, land, device = tile_y, 0, y_next[1]
        if source is None:
            src = ybuf.at[r, part, pl.ds(rows, RADIUS)]
        else:
            src = source.at[part, pl.ds(rows - RADIUS, RADIUS)]
        return pltpu.make_async_remote_copy(
            src_ref=src,
            dst_ref=ybuf.at[r, part, pl.ds(land, RADIUS)],
            send_sem=y_send.at[r, d, i],
            recv_sem=y_recv.at[r, d, i],
            device_id=device,
            device_id_type=MESH,
        )

    def x_copy(r, d):
        if d == 0:
            start, land, device = RADIUS, RADIUS + tile_x, x_prev[1]
        else:
            start, land, device = tile_x, 0, x_next[1]
        return pltpu.make_async_remote_copy(
            src_ref=xbuf.at[r, pl.ds(start, RADIUS)],
            dst_ref=xbuf.at[r, pl.ds(land, RADIUS)],
            send_sem=x_send.at[r, d],
            recv_sem=x_recv.at[r, d],
            device_id=device,
            device_id_type=MESH,
        )

    def s_copy(k, i):
        part = pl.ds(*pieces[i])
        return pltpu.make_async_remote_copy(
            src_ref=sens.at[me, part],
            dst_ref=sens.at[me, part],
            send_sem=s_send.at[k, i],
            recv_sem=s_recv.at[k, i],
            device_id=others[k],
            device_id_type=MESH,
        )

    def y_start(r, i, source=None):
        for d, (there, _) in enumerate((y_prev, y_next)):

            @pl.when(there)
            def _(d=d):
                y_copy(r, d, i, source).start()

    def y_arrive(r, i):
        for d, (there, _) in enumerate((y_next, y_prev)):

            @pl.when(there)
            def _(d=d):
                y_copy(r, d, i).wait_recv()

    for i in range(len(pieces)):
        y_start(0, i, den)

    for there, land in ((y_prev[0], 0), (y_next[0], RADIUS + tile_y)):

        @pl.when(jnp.logical_not(there))
        def _(land=land):
            for r in range(ROUNDS):
                ybuf[r, :, pl.ds(land, RADIUS)] = jnp.zeros(
                    (tile_x, RADIUS, depth), jnp.float32
                )

    for there, land in ((x_prev[0], 0), (x_next[0], RADIUS + tile_x)):

        @pl.when(jnp.logical_not(there))
        def _(land=land):
            for r in range(ROUNDS):
                xbuf[r, pl.ds(land, RADIUS)] = jnp.zeros(
                    (RADIUS, tile_y, depth), jnp.float32
                )

    group = RADIUS
    y_taps = plane_matrix(tile_y, group)
    z_taps = depth_matrix(depth)

    for i, (p, n) in enumerate(pieces):
        loads["f", i].wait()
        loads["a", i].wait()
        for q in range(p, p + n):
            total = None
            for s in range(sources):
                real, imag = None, None
                for c in range(comps):
                    a = fbuf[s, 0, c, q].astype(jnp.float32) * abuf[s, 0, c, q].astype(
                        jnp.float32
                    )
                    b = fbuf[s, 1, c, q].astype(jnp.float32) * abuf[s, 1, c, q].astype(
                        jnp.float32
                    )
                    real = (a - b) if real is None else real + (a - b)
                term = weight[s] * real
                total = term if total is None else total + term
            sens[me, q] = total
        for k in range(len(others)):
            s_copy(k, i).start()

    def y_filter(r, i):
        p, n = pieces[i]
        for g in range(p, p + n, group):
            value = ybuf[r, pl.ds(g, group)].reshape(
                group * (tile_y + 2 * RADIUS), depth
            )
            high, low = split(value)
            out = jnp.dot(y_taps, high, preferred_element_type=jnp.float32)
            out = out + jnp.dot(y_taps, low, preferred_element_type=jnp.float32)
            xbuf[r, pl.ds(RADIUS + g, group)] = out.reshape(group, tile_y, depth)

    def xz_filter(r, i):
        p, n = pieces[i]
        halves = []
        for h in range(0, tile_y, 8):
            value = xbuf[r, pl.ds(p, n + 2 * RADIUS), pl.ds(h, 8)]
            halves.append(box(box(value)))
        value = jnp.concatenate(halves, axis=1).reshape(n * tile_y, depth)
        both = jnp.concatenate(split(value), axis=1)
        out = jnp.dot(both, z_taps, preferred_element_type=jnp.float32)
        return (out * NORM).reshape(n, tile_y, depth)

    def through_x(r):
        for i in (0, 1):
            y_arrive(r, i)
            y_filter(r, i)
            there = (x_prev, x_next)[i][0]

            @pl.when(there)
            def _(i=i):
                x_copy(r, i).start()

        y_arrive(r, 2)
        y_filter(r, 2)

    def x_arrive(r, i):
        there = (x_prev, x_next)[i][0]

        @pl.when(there)
        def _():
            x_copy(r, 1 - i).wait_recv()

    def chain(i, filtered):
        p, n = pieces[i]
        part = pl.ds(p, n)
        for k in range(len(others)):
            source = lax.rem(me + n_illum - 1 - k, n_illum)
            pltpu.make_async_remote_copy(
                src_ref=sens.at[me, part],
                dst_ref=sens.at[source, part],
                send_sem=s_send.at[k, i],
                recv_sem=s_recv.at[k, i],
                device_id=others[k],
                device_id_type=MESH,
            ).wait_recv()
        total = sens[0, part]
        for e in range(1, n_illum):
            total = total + sens[e, part]
        inner = jnp.tanh(SHARPNESS * (filtered - THRESHOLD))
        ybuf[1, part, own] = total * (
            SHARPNESS * (1.0 - inner * inner) * (1.0 / SCALE)
        )
        y_start(1, i)

    def update(i, gradient):
        part = pl.ds(*pieces[i])
        one = 0.9 * m1buf[part] + 0.1 * gradient
        two = 0.999 * m2buf[part] + 0.001 * gradient * gradient
        m1buf[part] = one
        m2buf[part] = two
        step = one * FIRST_FIX / (jnp.sqrt(two * SECOND_FIX) + 1e-08)
        value = jnp.clip(ybuf[0, part, own] - 0.05 * step, 0.0, 1.0)
        ybuf[2, part, own] = value
        y_start(2, i)

    def finish(i, value):
        part = pl.ds(*pieces[i])
        pbuf[part] = (TANH_EDGE + jnp.tanh(SHARPNESS * (value - THRESHOLD))) * (
            1.0 / SCALE
        )
        pltpu.make_async_copy(pbuf.at[part], physical.at[part], out_sem.at[i]).start()

    loads["d"].wait()
    through_x(0)
    filt[...] = xz_filter(0, 2)
    for i in (0, 1):
        x_arrive(0, i)
        chain(i, xz_filter(0, i))
    chain(2, filt[...])

    loads["m1"].wait()
    loads["m2"].wait()
    through_x(1)
    filt[...] = xz_filter(1, 2)
    for i in (0, 1):
        x_arrive(1, i)
        update(i, xz_filter(1, i))
    update(2, filt[...])
    stores = [
        pltpu.make_async_copy(m1buf, new_m1, out_sem.at[3]),
        pltpu.make_async_copy(m2buf, new_m2, out_sem.at[4]),
        pltpu.make_async_copy(ybuf.at[2, :, own], new_den, out_sem.at[5]),
    ]
    for store in stores:
        store.start()

    through_x(2)
    finish(2, xz_filter(2, 2))
    for i in (0, 1):
        x_arrive(2, i)
        finish(i, xz_filter(2, i))

    for i, piece in enumerate(pieces):
        part = pl.ds(*piece)
        pltpu.make_async_copy(pbuf.at[part], physical.at[part], out_sem.at[i]).wait()
    for store in stores:
        store.wait()
    for i in range(len(pieces)):
        for k in range(len(others)):
            s_copy(k, i).wait_send()
    for d in (0, 1):

        @pl.when((y_prev, y_next)[d][0])
        def _(d=d):
            for r in range(ROUNDS):
                for i in range(len(pieces)):
                    y_copy(r, d, i, den if r == 0 else None).wait_send()

        @pl.when((x_prev, x_next)[d][0])
        def _(d=d):
            for r in range(ROUNDS):
                x_copy(r, d).wait_send()


def shards(sizes, density, moment_one, moment_two, forward_field, adjoint_field, objective_weight):
    tile_x, tile_y, depth = density.shape
    n_illum = sizes[0]
    tile = jax.ShapeDtypeStruct(density.shape, jnp.float32)
    f32 = jnp.float32
    far = max(n_illum - 1, 1)
    return pl.pallas_call(
        functools.partial(kernel, sizes),
        out_shape=(tile,) * 4,
        in_specs=[pl.BlockSpec(memory_space=pl.ANY)] * 5
        + [pl.BlockSpec(memory_space=pltpu.SMEM)],
        out_specs=(pl.BlockSpec(memory_space=pl.ANY),) * 4,
        scratch_shapes=[
            pltpu.VMEM((ROUNDS, tile_x, tile_y + 2 * RADIUS, depth), f32),
            pltpu.VMEM((ROUNDS, tile_x + 2 * RADIUS, tile_y, depth), f32),
            pltpu.VMEM((n_illum, tile_x, tile_y, depth), f32),
            pltpu.VMEM(forward_field.shape, forward_field.dtype),
            pltpu.VMEM(adjoint_field.shape, adjoint_field.dtype),
            pltpu.VMEM(density.shape, f32),
            pltpu.VMEM(density.shape, f32),
            pltpu.VMEM(density.shape, f32),
            pltpu.VMEM(density.shape, f32),
            pltpu.VMEM((tile_x - 2 * RADIUS, tile_y, depth), f32),
            pltpu.SemaphoreType.DMA((9,)),
            pltpu.SemaphoreType.DMA((6,)),
            pltpu.SemaphoreType.DMA((ROUNDS, 2, 3)),
            pltpu.SemaphoreType.DMA((ROUNDS, 2, 3)),
            pltpu.SemaphoreType.DMA((ROUNDS, 2)),
            pltpu.SemaphoreType.DMA((ROUNDS, 2)),
            pltpu.SemaphoreType.DMA((far, 3)),
            pltpu.SemaphoreType.DMA((far, 3)),
        ],
        compiler_params=pltpu.CompilerParams(collective_id=0, has_side_effects=True),
        name="design_update",
    )(density, moment_one, moment_two, forward_field, adjoint_field, objective_weight)


def solution(mesh):
    field = P("illum", None, None, "gx", "gy", None)
    tile = P("gx", "gy", None)
    sizes = (mesh.shape["illum"], mesh.shape["gx"], mesh.shape["gy"])
    return jax.shard_map(
        functools.partial(shards, sizes),
        mesh=mesh,
        in_specs=(tile, tile, tile, field, field, P("illum")),
        out_specs=(tile,) * 4,
        check_vma=False,
    )
```

```python
import functools
import math

import jax
import jax.numpy as jnp
from jax import lax
from jax.experimental import pallas as pl
from jax.experimental.pallas import tpu as pltpu
from jax.sharding import PartitionSpec as P

RADIUS = 8
SHARPNESS = 8.0
THRESHOLD = 0.5
TANH_EDGE = math.tanh(SHARPNESS * THRESHOLD)
SCALE = math.tanh(SHARPNESS * THRESHOLD) + math.tanh(SHARPNESS * (1.0 - THRESHOLD))
NORM = 1.0 / float((RADIUS + 1) ** 6)
FIRST_FIX = 1.0 / (1.0 - 0.9**5)
SECOND_FIX = 1.0 / (1.0 - 0.999**5)
MESH = pl.DeviceIdType.MESH
ROUNDS = 3


def split(value):
    high = value.astype(jnp.bfloat16)
    low = (value - high.astype(jnp.float32)).astype(jnp.bfloat16)
    return high, low


def box(value):
    n = value.shape[0]
    two = value[: n - 1] + value[1:]
    four = two[: n - 3] + two[2:]
    eight = four[: n - 7] + four[4:]
    return eight[: n - 8] + value[8:]


def plane_matrix(tile_y, group):
    rows, cols = group * tile_y, group * (tile_y + 2 * RADIUS)
    row = lax.broadcasted_iota(jnp.int32, (rows, cols), 0)
    col = lax.broadcasted_iota(jnp.int32, (rows, cols), 1)
    padded = tile_y + 2 * RADIUS
    plane = row // tile_y
    apart = jnp.abs((col - plane * padded) - (row - plane * tile_y) - RADIUS)
    taps = jnp.maximum(RADIUS + 1 - apart, 0)
    return taps.astype(jnp.float32).astype(jnp.bfloat16)


def depth_matrix(length):
    row = lax.broadcasted_iota(jnp.int32, (2 * length, length), 0)
    col = lax.broadcasted_iota(jnp.int32, (2 * length, length), 1)
    row = jnp.where(row >= length, row - length, row)
    taps = jnp.maximum(RADIUS + 1 - jnp.abs(row - col), 0)
    return taps.astype(jnp.float32).astype(jnp.bfloat16)


def kernel(
    sizes,
    den,
    m1,
    m2,
    fwd,
    adj,
    weight,
    new_den,
    new_m1,
    new_m2,
    physical,
    ybuf,
    xbuf,
    sens,
    fbuf,
    abuf,
    m1buf,
    m2buf,
    wbuf,
    filt,
    local_sem,
    y_send,
    y_recv,
    x_send,
    x_recv,
    s_send,
    s_recv,
):
    n_illum, n_gx, n_gy = sizes
    tile_x, tile_y, depth = den.shape
    sources, _, comps = fwd.shape[:3]
    me = lax.axis_index("illum")
    gx = lax.axis_index("gx")
    gy = lax.axis_index("gy")
    side = (gx < n_gx // 2).astype(jnp.int32)
    reach = tile_x - RADIUS
    pieces = [
        (side * reach, RADIUS),
        ((1 - side) * reach, RADIUS),
        (RADIUS, tile_x - 2 * RADIUS),
    ]
    own = pl.ds(RADIUS, tile_y)

    loads = {}

    def load(name, src, dst):
        copy = pltpu.make_async_copy(src, dst, local_sem.at[len(loads)])
        copy.start()
        loads[name] = copy

    for i, (p, n) in enumerate(pieces):
        part = pl.ds(p, n)
        load(("f", i), fwd.at[:, :, :, part], fbuf.at[:, :, :, part])
        load(("a", i), adj.at[:, :, :, part], abuf.at[:, :, :, part])
    load("w", weight, wbuf)
    load("d", den, ybuf.at[0, :, own])
    load("m1", m1, m1buf)
    load("m2", m2, m2buf)

    near, far = gx + 2 * side - 1, gx - 2 * side + 1
    x_sides = [
        (jnp.logical_and(at >= 0, at < n_gx), {"gx": jnp.clip(at, 0, n_gx - 1)})
        for at in (near, far)
    ]
    y_prev = (gy > 0, {"gy": jnp.maximum(gy - 1, 0)})
    y_next = (gy < n_gy - 1, {"gy": jnp.minimum(gy + 1, n_gy - 1)})
    others = [{"illum": lax.rem(me + k, n_illum)} for k in range(1, n_illum)]

    barrier = pltpu.get_barrier_semaphore()
    for there, device in (y_prev, y_next, *x_sides):

        @pl.when(there)
        def _(device=device):
            pl.semaphore_signal(barrier, inc=1, device_id=device, device_id_type=MESH)

    for device in others:
        pl.semaphore_signal(barrier, inc=1, device_id=device, device_id_type=MESH)
    for there, land in ((y_prev[0], 0), (y_next[0], RADIUS + tile_y)):

        @pl.when(jnp.logical_not(there))
        def _(land=land):
            for r in range(ROUNDS):
                ybuf[r, :, pl.ds(land, RADIUS)] = jnp.zeros(
                    (tile_x, RADIUS, depth), jnp.float32
                )

    for there, land in ((gx > 0, 0), (gx < n_gx - 1, RADIUS + tile_x)):

        @pl.when(jnp.logical_not(there))
        def _(land=land):
            for r in range(ROUNDS):
                xbuf[r, pl.ds(land, RADIUS)] = jnp.zeros(
                    (RADIUS, tile_y, depth), jnp.float32
                )

    group = RADIUS
    y_taps = plane_matrix(tile_y, group)
    z_taps = depth_matrix(depth)

    peers = jnp.int32(len(others))
    for there, _ in (y_prev, y_next, *x_sides):
        peers = peers + there.astype(jnp.int32)
    pl.semaphore_wait(barrier, peers)

    def y_copy(r, d, i, source=None):
        p, n = pieces[i]
        part = pl.ds(p, n)
        if d == 0:
            rows, land, device = RADIUS, RADIUS + tile_y, y_prev[1]
        else:
            rows, land, device = tile_y, 0, y_next[1]
        if source is None:
            src = ybuf.at[r, part, pl.ds(rows, RADIUS)]
        else:
            src = source.at[part, pl.ds(rows - RADIUS, RADIUS)]
        return pltpu.make_async_remote_copy(
            src_ref=src,
            dst_ref=ybuf.at[r, part, pl.ds(land, RADIUS)],
            send_sem=y_send.at[r, d, i],
            recv_sem=y_recv.at[r, d, i],
            device_id=device,
            device_id_type=MESH,
        )

    def x_copy(r, i, back=False):
        start = pieces[i][0]
        high = side if i == 0 else 1 - side
        if back:
            land = high * (tile_x + RADIUS)
        else:
            land = (1 - high) * (tile_x + RADIUS)
        sent, got = (1 - high, high)
        return pltpu.make_async_remote_copy(
            src_ref=xbuf.at[r, pl.ds(RADIUS + start, RADIUS)],
            dst_ref=xbuf.at[r, pl.ds(land, RADIUS)],
            send_sem=x_send.at[r, i],
            recv_sem=x_recv.at[r, got if back else sent],
            device_id=x_sides[i][1],
            device_id_type=MESH,
        )

    def s_copy(k, i):
        part = pl.ds(*pieces[i])
        return pltpu.make_async_remote_copy(
            src_ref=sens.at[me, part],
            dst_ref=sens.at[me, part],
            send_sem=s_send.at[k, i],
            recv_sem=s_recv.at[k, i],
            device_id=others[k],
            device_id_type=MESH,
        )

    def y_start(r, i, source=None):
        for d, (there, _) in enumerate((y_prev, y_next)):

            @pl.when(there)
            def _(d=d):
                y_copy(r, d, i, source).start()

    def y_arrive(r, i):
        for d, (there, _) in enumerate((y_next, y_prev)):

            @pl.when(there)
            def _(d=d):
                y_copy(r, d, i).wait_recv()

    for i in range(len(pieces)):
        y_start(0, i, den)

    loads["w"].wait()

    for i, (p, n) in enumerate(pieces):
        loads["f", i].wait()
        loads["a", i].wait()
        for q in [p + j for j in range(n)]:
            total = None
            for s in range(sources):
                real, imag = None, None
                for c in range(comps):
                    a = fbuf[s, 0, c, q].astype(jnp.float32) * abuf[s, 0, c, q].astype(
                        jnp.float32
                    )
                    b = fbuf[s, 1, c, q].astype(jnp.float32) * abuf[s, 1, c, q].astype(
                        jnp.float32
                    )
                    real = (a - b) if real is None else real + (a - b)
                term = wbuf[s] * real
                total = term if total is None else total + term
            sens[me, q] = total
        for k in range(len(others)):
            s_copy(k, i).start()

    def y_filter(r, i):
        p, n = pieces[i]
        for g in [p + j for j in range(0, n, group)]:
            value = ybuf[r, pl.ds(g, group)].reshape(
                group * (tile_y + 2 * RADIUS), depth
            )
            high, low = split(value)
            out = jnp.dot(y_taps, high, preferred_element_type=jnp.float32)
            out = out + jnp.dot(y_taps, low, preferred_element_type=jnp.float32)
            xbuf[r, pl.ds(RADIUS + g, group)] = out.reshape(group, tile_y, depth)

    def xz_filter(r, i):
        p, n = pieces[i]
        halves = []
        for h in range(0, tile_y, 8):
            value = xbuf[r, pl.ds(p, n + 2 * RADIUS), pl.ds(h, 8)]
            halves.append(box(box(value)))
        value = jnp.concatenate(halves, axis=1).reshape(n * tile_y, depth)
        both = jnp.concatenate(split(value), axis=1)
        out = jnp.dot(both, z_taps, preferred_element_type=jnp.float32)
        return (out * NORM).reshape(n, tile_y, depth)

    def through_x(r):
        for i in (0, 1):
            y_arrive(r, i)
            y_filter(r, i)
            there = x_sides[i][0]

            @pl.when(there)
            def _(i=i):
                x_copy(r, i).start()

        y_arrive(r, 2)
        y_filter(r, 2)

    def x_arrive(r, i):
        there = x_sides[i][0]

        @pl.when(there)
        def _():
            x_copy(r, i, back=True).wait_recv()

    def chain(i, filtered):
        p, n = pieces[i]
        part = pl.ds(p, n)
        for k in range(len(others)):
            source = lax.rem(me + n_illum - 1 - k, n_illum)
            pltpu.make_async_remote_copy(
                src_ref=sens.at[me, part],
                dst_ref=sens.at[source, part],
                send_sem=s_send.at[k, i],
                recv_sem=s_recv.at[k, i],
                device_id=others[k],
                device_id_type=MESH,
            ).wait_recv()
        total = sens[0, part]
        for e in range(1, n_illum):
            total = total + sens[e, part]
        inner = jnp.tanh(SHARPNESS * (filtered - THRESHOLD))
        ybuf[1, part, own] = total * (
            SHARPNESS * (1.0 - inner * inner) * (1.0 / SCALE)
        )
        y_start(1, i)

    def update(i, gradient):
        part = pl.ds(*pieces[i])
        one = 0.9 * m1buf[part] + 0.1 * gradient
        two = 0.999 * m2buf[part] + 0.001 * gradient * gradient
        new_m1[part] = one
        new_m2[part] = two
        step = one * FIRST_FIX / (jnp.sqrt(two * SECOND_FIX) + 1e-08)
        value = jnp.clip(ybuf[0, part, own] - 0.05 * step, 0.0, 1.0)
        ybuf[2, part, own] = value
        y_start(2, i)
        new_den[part] = value

    def finish(i, value):
        part = pl.ds(*pieces[i])
        physical[part] = (TANH_EDGE + jnp.tanh(SHARPNESS * (value - THRESHOLD))) * (
            1.0 / SCALE
        )

    loads["d"].wait()
    through_x(0)
    filt[...] = xz_filter(0, 2)
    for i in (0, 1):
        x_arrive(0, i)
        chain(i, xz_filter(0, i))
    chain(2, filt[...])

    loads["m1"].wait()
    loads["m2"].wait()
    through_x(1)
    filt[...] = xz_filter(1, 2)
    for i in (0, 1):
        x_arrive(1, i)
        update(i, xz_filter(1, i))
    update(2, filt[...])
    through_x(2)
    finish(2, xz_filter(2, 2))
    for i in (0, 1):
        x_arrive(2, i)
        finish(i, xz_filter(2, i))

    for i in range(len(pieces)):
        for k in range(len(others)):
            s_copy(k, i).wait_send()
    for d in (0, 1):

        @pl.when((y_prev, y_next)[d][0])
        def _(d=d):
            for r in range(ROUNDS):
                for i in range(len(pieces)):
                    y_copy(r, d, i, den if r == 0 else None).wait_send()

        @pl.when(x_sides[d][0])
        def _(d=d):
            for r in range(ROUNDS):
                x_copy(r, d).wait_send()


def export(a, b, c, d, a_out, b_out, c_out, d_out, sem):
    copies = [
        pltpu.make_async_copy(src, dst, sem.at[i])
        for i, (src, dst) in enumerate(
            ((a, a_out), (b, b_out), (c, c_out), (d, d_out))
        )
    ]
    for copy in copies:
        copy.start()
    for copy in copies:
        copy.wait()


def shards(sizes, density, moment_one, moment_two, forward_field, adjoint_field, objective_weight):
    tile_x, tile_y, depth = density.shape
    n_illum = sizes[0]
    tile = jax.ShapeDtypeStruct(density.shape, jnp.float32)
    f32 = jnp.float32
    far = max(n_illum - 1, 1)
    results = pl.pallas_call(
        functools.partial(kernel, sizes),
        out_shape=(pltpu.VMEM(density.shape, f32),) * 4,
        in_specs=[pl.BlockSpec(memory_space=pltpu.HBM)] * 6,
        out_specs=(pl.BlockSpec(memory_space=pltpu.VMEM),) * 4,
        scratch_shapes=[
            pltpu.VMEM((ROUNDS, tile_x, tile_y + 2 * RADIUS, depth), f32),
            pltpu.VMEM((ROUNDS, tile_x + 2 * RADIUS, tile_y, depth), f32),
            pltpu.VMEM((n_illum, tile_x, tile_y, depth), f32),
            pltpu.VMEM(forward_field.shape, forward_field.dtype),
            pltpu.VMEM(adjoint_field.shape, adjoint_field.dtype),
            pltpu.VMEM(density.shape, f32),
            pltpu.VMEM(density.shape, f32),
            pltpu.SMEM(objective_weight.shape, f32),
            pltpu.VMEM((tile_x - 2 * RADIUS, tile_y, depth), f32),
            pltpu.SemaphoreType.DMA((10,)),
            pltpu.SemaphoreType.DMA((ROUNDS, 2, 3)),
            pltpu.SemaphoreType.DMA((ROUNDS, 2, 3)),
            pltpu.SemaphoreType.DMA((ROUNDS, 2)),
            pltpu.SemaphoreType.DMA((ROUNDS, 2)),
            pltpu.SemaphoreType.DMA((far, 3)),
            pltpu.SemaphoreType.DMA((far, 3)),
        ],
        compiler_params=pltpu.CompilerParams(
            collective_id=0, has_side_effects=True, vmem_limit_bytes=48 << 20
        ),
        name="design_update",
    )(density, moment_one, moment_two, forward_field, adjoint_field, objective_weight)
    return pl.pallas_call(
        export,
        out_shape=(tile,) * 4,
        in_specs=[pl.BlockSpec(memory_space=pltpu.VMEM)] * 4,
        out_specs=(pl.BlockSpec(memory_space=pl.ANY),) * 4,
        scratch_shapes=[pltpu.SemaphoreType.DMA((4,))],
        compiler_params=pltpu.CompilerParams(vmem_limit_bytes=4 << 20),
        name="export_results",
    )(*results)


def solution(mesh):
    field = P("illum", None, None, "gx", "gy", None)
    tile = P("gx", "gy", None)
    sizes = (mesh.shape["illum"], mesh.shape["gx"], mesh.shape["gy"])
    return jax.shard_map(
        functools.partial(shards, sizes),
        mesh=mesh,
        in_specs=(tile, tile, tile, field, field, P("illum")),
        out_specs=(tile,) * 4,
        check_vma=False,
    )
```

```python
import functools
import math

import jax
import jax.numpy as jnp
from jax import lax
from jax.experimental import pallas as pl
from jax.experimental.pallas import tpu as pltpu
from jax.sharding import PartitionSpec as P

RADIUS = 8
SHARPNESS = 8.0
THRESHOLD = 0.5
TANH_EDGE = math.tanh(SHARPNESS * THRESHOLD)
SCALE = math.tanh(SHARPNESS * THRESHOLD) + math.tanh(SHARPNESS * (1.0 - THRESHOLD))
NORM = 1.0 / float((RADIUS + 1) ** 6)
FIRST_FIX = 1.0 / (1.0 - 0.9**5)
SECOND_FIX = 1.0 / (1.0 - 0.999**5)
MESH = pl.DeviceIdType.MESH
ROUNDS = 3


def split(value):
    high = value.astype(jnp.bfloat16)
    low = (value - high.astype(jnp.float32)).astype(jnp.bfloat16)
    return high, low


def box(value):
    n = value.shape[0]
    two = value[: n - 1] + value[1:]
    four = two[: n - 3] + two[2:]
    eight = four[: n - 7] + four[4:]
    return eight[: n - 8] + value[8:]


def plane_matrix(tile_y, group):
    rows, cols = group * tile_y, group * (tile_y + 2 * RADIUS)
    row = lax.broadcasted_iota(jnp.int32, (rows, cols), 0)
    col = lax.broadcasted_iota(jnp.int32, (rows, cols), 1)
    padded = tile_y + 2 * RADIUS
    plane = row // tile_y
    apart = jnp.abs((col - plane * padded) - (row - plane * tile_y) - RADIUS)
    taps = jnp.maximum(RADIUS + 1 - apart, 0)
    return taps.astype(jnp.float32).astype(jnp.bfloat16)


def depth_matrix(length):
    row = lax.broadcasted_iota(jnp.int32, (2 * length, length), 0)
    col = lax.broadcasted_iota(jnp.int32, (2 * length, length), 1)
    row = jnp.where(row >= length, row - length, row)
    taps = jnp.maximum(RADIUS + 1 - jnp.abs(row - col), 0)
    return taps.astype(jnp.float32).astype(jnp.bfloat16)


def kernel(
    sizes,
    den,
    m1,
    m2,
    fwd,
    adj,
    weight,
    new_den,
    new_m1,
    new_m2,
    physical,
    ybuf,
    xbuf,
    sens,
    fbuf,
    abuf,
    m1buf,
    m2buf,
    filt,
    local_sem,
    y_send,
    y_recv,
    x_send,
    x_recv,
    s_send,
    s_recv,
):
    n_illum, n_gx, n_gy = sizes
    tile_x, tile_y, depth = den.shape
    sources, _, comps = fwd.shape[:3]
    me = lax.axis_index("illum")
    gx = lax.axis_index("gx")
    gy = lax.axis_index("gy")
    side = (gx < n_gx // 2).astype(jnp.int32)
    reach = tile_x - RADIUS
    pieces = [
        (side * reach, RADIUS),
        ((1 - side) * reach, RADIUS),
        (RADIUS, tile_x - 2 * RADIUS),
    ]
    own = pl.ds(RADIUS, tile_y)

    loads = {}

    def load(name, src, dst):
        copy = pltpu.make_async_copy(src, dst, local_sem.at[len(loads)])
        copy.start()
        loads[name] = copy

    for i, (p, n) in enumerate(pieces):
        part = pl.ds(p, n)
        load(("f", i), fwd.at[:, :, :, part], fbuf.at[:, :, :, part])
        load(("a", i), adj.at[:, :, :, part], abuf.at[:, :, :, part])
    load("d", den, ybuf.at[0, :, own])
    load("m1", m1, m1buf)
    load("m2", m2, m2buf)

    near, far = gx + 2 * side - 1, gx - 2 * side + 1
    x_sides = [
        (jnp.logical_and(at >= 0, at < n_gx), {"gx": jnp.clip(at, 0, n_gx - 1)})
        for at in (near, far)
    ]
    y_prev = (gy > 0, {"gy": jnp.maximum(gy - 1, 0)})
    y_next = (gy < n_gy - 1, {"gy": jnp.minimum(gy + 1, n_gy - 1)})
    others = [{"illum": lax.rem(me + k, n_illum)} for k in range(1, n_illum)]

    barrier = pltpu.get_barrier_semaphore()
    for there, device in (y_prev, y_next, *x_sides):

        @pl.when(there)
        def _(device=device):
            pl.semaphore_signal(barrier, inc=1, device_id=device, device_id_type=MESH)

    for device in others:
        pl.semaphore_signal(barrier, inc=1, device_id=device, device_id_type=MESH)
    for there, land in ((y_prev[0], 0), (y_next[0], RADIUS + tile_y)):

        @pl.when(jnp.logical_not(there))
        def _(land=land):
            for r in range(ROUNDS):
                ybuf[r, :, pl.ds(land, RADIUS)] = jnp.zeros(
                    (tile_x, RADIUS, depth), jnp.float32
                )

    for there, land in ((gx > 0, 0), (gx < n_gx - 1, RADIUS + tile_x)):

        @pl.when(jnp.logical_not(there))
        def _(land=land):
            for r in range(ROUNDS):
                xbuf[r, pl.ds(land, RADIUS)] = jnp.zeros(
                    (RADIUS, tile_y, depth), jnp.float32
                )

    group = RADIUS
    y_taps = plane_matrix(tile_y, group)
    z_taps = depth_matrix(depth)

    peers = jnp.int32(len(others))
    for there, _ in (y_prev, y_next, *x_sides):
        peers = peers + there.astype(jnp.int32)
    pl.semaphore_wait(barrier, peers)

    def y_copy(r, d, i, source=None):
        p, n = pieces[i]
        part = pl.ds(p, n)
        if d == 0:
            rows, land, device = RADIUS, RADIUS + tile_y, y_prev[1]
        else:
            rows, land, device = tile_y, 0, y_next[1]
        if source is None:
            src = ybuf.at[r, part, pl.ds(rows, RADIUS)]
        else:
            src = source.at[part, pl.ds(rows - RADIUS, RADIUS)]
        return pltpu.make_async_remote_copy(
            src_ref=src,
            dst_ref=ybuf.at[r, part, pl.ds(land, RADIUS)],
            send_sem=y_send.at[r, d, i],
            recv_sem=y_recv.at[r, d, i],
            device_id=device,
            device_id_type=MESH,
        )

    def x_copy(r, i, back=False):
        start = pieces[i][0]
        high = side if i == 0 else 1 - side
        if back:
            land = high * (tile_x + RADIUS)
        else:
            land = (1 - high) * (tile_x + RADIUS)
        sent, got = (1 - high, high)
        return pltpu.make_async_remote_copy(
            src_ref=xbuf.at[r, pl.ds(RADIUS + start, RADIUS)],
            dst_ref=xbuf.at[r, pl.ds(land, RADIUS)],
            send_sem=x_send.at[r, i],
            recv_sem=x_recv.at[r, got if back else sent],
            device_id=x_sides[i][1],
            device_id_type=MESH,
        )

    def s_copy(k, i):
        part = pl.ds(*pieces[i])
        return pltpu.make_async_remote_copy(
            src_ref=sens.at[me, part],
            dst_ref=sens.at[me, part],
            send_sem=s_send.at[k, i],
            recv_sem=s_recv.at[k, i],
            device_id=others[k],
            device_id_type=MESH,
        )

    def y_start(r, i, source=None):
        for d, (there, _) in enumerate((y_prev, y_next)):

            @pl.when(there)
            def _(d=d):
                y_copy(r, d, i, source).start()

    def y_arrive(r, i):
        for d, (there, _) in enumerate((y_next, y_prev)):

            @pl.when(there)
            def _(d=d):
                y_copy(r, d, i).wait_recv()

    for i in range(len(pieces)):
        y_start(0, i, den)

    for i, (p, n) in enumerate(pieces):
        loads["f", i].wait()
        loads["a", i].wait()
        for q in [p + j for j in range(n)]:
            total = None
            for s in range(sources):
                real, imag = None, None
                for c in range(comps):
                    a = fbuf[s, 0, c, q].astype(jnp.float32) * abuf[s, 0, c, q].astype(
                        jnp.float32
                    )
                    b = fbuf[s, 1, c, q].astype(jnp.float32) * abuf[s, 1, c, q].astype(
                        jnp.float32
                    )
                    real = (a - b) if real is None else real + (a - b)
                term = weight[s] * real
                total = term if total is None else total + term
            sens[me, q] = total
        for k in range(len(others)):
            s_copy(k, i).start()

    def y_filter(r, i):
        p, n = pieces[i]
        for g in [p + j for j in range(0, n, group)]:
            value = ybuf[r, pl.ds(g, group)].reshape(
                group * (tile_y + 2 * RADIUS), depth
            )
            high, low = split(value)
            out = jnp.dot(y_taps, high, preferred_element_type=jnp.float32)
            out = out + jnp.dot(y_taps, low, preferred_element_type=jnp.float32)
            xbuf[r, pl.ds(RADIUS + g, group)] = out.reshape(group, tile_y, depth)

    def xz_filter(r, i):
        p, n = pieces[i]
        halves = []
        for h in range(0, tile_y, 8):
            value = xbuf[r, pl.ds(p, n + 2 * RADIUS), pl.ds(h, 8)]
            halves.append(box(box(value)))
        value = jnp.concatenate(halves, axis=1).reshape(n * tile_y, depth)
        both = jnp.concatenate(split(value), axis=1)
        out = jnp.dot(both, z_taps, preferred_element_type=jnp.float32)
        return (out * NORM).reshape(n, tile_y, depth)

    def through_x(r):
        for i in (0, 1):
            y_arrive(r, i)
            y_filter(r, i)
            there = x_sides[i][0]

            @pl.when(there)
            def _(i=i):
                x_copy(r, i).start()

        y_arrive(r, 2)
        y_filter(r, 2)

    def x_arrive(r, i):
        there = x_sides[i][0]

        @pl.when(there)
        def _():
            x_copy(r, i, back=True).wait_recv()

    def chain(i, filtered):
        p, n = pieces[i]
        part = pl.ds(p, n)
        for k in range(len(others)):
            source = lax.rem(me + n_illum - 1 - k, n_illum)
            pltpu.make_async_remote_copy(
                src_ref=sens.at[me, part],
                dst_ref=sens.at[source, part],
                send_sem=s_send.at[k, i],
                recv_sem=s_recv.at[k, i],
                device_id=others[k],
                device_id_type=MESH,
            ).wait_recv()
        total = sens[0, part]
        for e in range(1, n_illum):
            total = total + sens[e, part]
        inner = jnp.tanh(SHARPNESS * (filtered - THRESHOLD))
        ybuf[1, part, own] = total * (
            SHARPNESS * (1.0 - inner * inner) * (1.0 / SCALE)
        )
        y_start(1, i)

    def update(i, gradient):
        part = pl.ds(*pieces[i])
        one = 0.9 * m1buf[part] + 0.1 * gradient
        two = 0.999 * m2buf[part] + 0.001 * gradient * gradient
        new_m1[part] = one
        new_m2[part] = two
        step = one * FIRST_FIX / (jnp.sqrt(two * SECOND_FIX) + 1e-08)
        value = jnp.clip(ybuf[0, part, own] - 0.05 * step, 0.0, 1.0)
        ybuf[2, part, own] = value
        y_start(2, i)
        new_den[part] = value

    def finish(i, value):
        part = pl.ds(*pieces[i])
        physical[part] = (TANH_EDGE + jnp.tanh(SHARPNESS * (value - THRESHOLD))) * (
            1.0 / SCALE
        )

    loads["d"].wait()
    through_x(0)
    filt[...] = xz_filter(0, 2)
    for i in (0, 1):
        x_arrive(0, i)
        chain(i, xz_filter(0, i))
    chain(2, filt[...])

    loads["m1"].wait()
    loads["m2"].wait()
    through_x(1)
    filt[...] = xz_filter(1, 2)
    for i in (0, 1):
        x_arrive(1, i)
        update(i, xz_filter(1, i))
    update(2, filt[...])
    through_x(2)
    finish(2, xz_filter(2, 2))
    for i in (0, 1):
        x_arrive(2, i)
        finish(i, xz_filter(2, i))

    for i in range(len(pieces)):
        for k in range(len(others)):
            s_copy(k, i).wait_send()
    for d in (0, 1):

        @pl.when((y_prev, y_next)[d][0])
        def _(d=d):
            for r in range(ROUNDS):
                for i in range(len(pieces)):
                    y_copy(r, d, i, den if r == 0 else None).wait_send()

        @pl.when(x_sides[d][0])
        def _(d=d):
            for r in range(ROUNDS):
                x_copy(r, d).wait_send()


def export(a, b, c, d, a_out, b_out, c_out, d_out, sem):
    copies = [
        pltpu.make_async_copy(src, dst, sem.at[i])
        for i, (src, dst) in enumerate(
            ((a, a_out), (b, b_out), (c, c_out), (d, d_out))
        )
    ]
    for copy in copies:
        copy.start()
    for copy in copies:
        copy.wait()


def shards(sizes, density, moment_one, moment_two, forward_field, adjoint_field, objective_weight):
    tile_x, tile_y, depth = density.shape
    n_illum = sizes[0]
    tile = jax.ShapeDtypeStruct(density.shape, jnp.float32)
    f32 = jnp.float32
    far = max(n_illum - 1, 1)
    arguments = [
        pltpu.with_memory_space_constraint(x, pltpu.HBM)
        for x in (density, moment_one, moment_two, forward_field, adjoint_field)
    ]
    results = pl.pallas_call(
        functools.partial(kernel, sizes),
        out_shape=(pltpu.VMEM(density.shape, f32),) * 4,
        in_specs=[pl.BlockSpec(memory_space=pltpu.HBM)] * 5
        + [pl.BlockSpec(memory_space=pltpu.SMEM)],
        out_specs=(pl.BlockSpec(memory_space=pltpu.VMEM),) * 4,
        scratch_shapes=[
            pltpu.VMEM((ROUNDS, tile_x, tile_y + 2 * RADIUS, depth), f32),
            pltpu.VMEM((ROUNDS, tile_x + 2 * RADIUS, tile_y, depth), f32),
            pltpu.VMEM((n_illum, tile_x, tile_y, depth), f32),
            pltpu.VMEM(forward_field.shape, forward_field.dtype),
            pltpu.VMEM(adjoint_field.shape, adjoint_field.dtype),
            pltpu.VMEM(density.shape, f32),
            pltpu.VMEM(density.shape, f32),
            pltpu.VMEM((tile_x - 2 * RADIUS, tile_y, depth), f32),
            pltpu.SemaphoreType.DMA((9,)),
            pltpu.SemaphoreType.DMA((ROUNDS, 2, 3)),
            pltpu.SemaphoreType.DMA((ROUNDS, 2, 3)),
            pltpu.SemaphoreType.DMA((ROUNDS, 2)),
            pltpu.SemaphoreType.DMA((ROUNDS, 2)),
            pltpu.SemaphoreType.DMA((far, 3)),
            pltpu.SemaphoreType.DMA((far, 3)),
        ],
        compiler_params=pltpu.CompilerParams(
            collective_id=0, has_side_effects=True, vmem_limit_bytes=48 << 20
        ),
        name="design_update",
    )(*arguments, objective_weight)
    return pl.pallas_call(
        export,
        out_shape=(tile,) * 4,
        in_specs=[pl.BlockSpec(memory_space=pltpu.VMEM)] * 4,
        out_specs=(pl.BlockSpec(memory_space=pl.ANY),) * 4,
        scratch_shapes=[pltpu.SemaphoreType.DMA((4,))],
        compiler_params=pltpu.CompilerParams(vmem_limit_bytes=4 << 20),
        name="export_results",
    )(*results)


def solution(mesh):
    field = P("illum", None, None, "gx", "gy", None)
    tile = P("gx", "gy", None)
    sizes = (mesh.shape["illum"], mesh.shape["gx"], mesh.shape["gy"])
    return jax.shard_map(
        functools.partial(shards, sizes),
        mesh=mesh,
        in_specs=(tile, tile, tile, field, field, P("illum")),
        out_specs=(tile,) * 4,
        check_vma=False,
    )
```

```python
import functools
import math

import jax
import jax.numpy as jnp
from jax import lax
from jax.experimental import pallas as pl
from jax.experimental.pallas import tpu as pltpu
from jax.sharding import PartitionSpec as P

RADIUS = 8
SHARPNESS = 8.0
THRESHOLD = 0.5
TANH_EDGE = math.tanh(SHARPNESS * THRESHOLD)
SCALE = math.tanh(SHARPNESS * THRESHOLD) + math.tanh(SHARPNESS * (1.0 - THRESHOLD))
NORM = 1.0 / float((RADIUS + 1) ** 6)
FIRST_FIX = 1.0 / (1.0 - 0.9**5)
SECOND_FIX = 1.0 / (1.0 - 0.999**5)
MESH = pl.DeviceIdType.MESH
ROUNDS = 3


def split(value):
    high = value.astype(jnp.bfloat16)
    low = (value - high.astype(jnp.float32)).astype(jnp.bfloat16)
    return high, low


def box(value):
    n = value.shape[0]
    two = value[: n - 1] + value[1:]
    four = two[: n - 3] + two[2:]
    eight = four[: n - 7] + four[4:]
    return eight[: n - 8] + value[8:]


def depth_matrix(length):
    row = lax.broadcasted_iota(jnp.int32, (2 * length, length), 0)
    col = lax.broadcasted_iota(jnp.int32, (2 * length, length), 1)
    row = jnp.where(row >= length, row - length, row)
    taps = jnp.maximum(RADIUS + 1 - jnp.abs(row - col), 0)
    return taps.astype(jnp.float32).astype(jnp.bfloat16)


def kernel(
    sizes,
    den,
    m1,
    m2,
    fwd,
    adj,
    weight,
    new_den,
    new_m1,
    new_m2,
    physical,
    ybuf,
    xbuf,
    sens,
    fbuf,
    abuf,
    m1buf,
    m2buf,
    filt,
    local_sem,
    y_send,
    y_recv,
    x_send,
    x_recv,
    s_send,
    s_recv,
):
    n_illum, n_gx, n_gy = sizes
    tile_x, tile_y, depth = den.shape
    sources, _, comps = fwd.shape[:3]
    me = lax.axis_index("illum")
    gx = lax.axis_index("gx")
    gy = lax.axis_index("gy")
    side = (gx < n_gx // 2).astype(jnp.int32)
    reach = tile_x - RADIUS
    pieces = [
        (side * reach, RADIUS),
        ((1 - side) * reach, RADIUS),
        (RADIUS, tile_x - 2 * RADIUS),
    ]
    own = pl.ds(RADIUS, tile_y)

    loads = {}

    def load(name, src, dst):
        copy = pltpu.make_async_copy(src, dst, local_sem.at[len(loads)])
        copy.start()
        loads[name] = copy

    for i, (p, n) in enumerate(pieces):
        part = pl.ds(p, n)
        load(("f", i), fwd.at[:, :, :, part], fbuf.at[:, :, :, part])
        load(("a", i), adj.at[:, :, :, part], abuf.at[:, :, :, part])
    load("d", den, ybuf.at[0, :, own])
    load("m1", m1, m1buf)
    load("m2", m2, m2buf)

    near, far = gx + 2 * side - 1, gx - 2 * side + 1
    x_sides = [
        (jnp.logical_and(at >= 0, at < n_gx), {"gx": jnp.clip(at, 0, n_gx - 1)})
        for at in (near, far)
    ]
    y_prev = (gy > 0, {"gy": jnp.maximum(gy - 1, 0)})
    y_next = (gy < n_gy - 1, {"gy": jnp.minimum(gy + 1, n_gy - 1)})
    others = [{"illum": lax.rem(me + k, n_illum)} for k in range(1, n_illum)]

    barrier = pltpu.get_barrier_semaphore()
    for there, device in (y_prev, y_next, *x_sides):

        @pl.when(there)
        def _(device=device):
            pl.semaphore_signal(barrier, inc=1, device_id=device, device_id_type=MESH)

    for device in others:
        pl.semaphore_signal(barrier, inc=1, device_id=device, device_id_type=MESH)
    for there, land in ((y_prev[0], 0), (y_next[0], RADIUS + tile_y)):

        @pl.when(jnp.logical_not(there))
        def _(land=land):
            for r in range(ROUNDS):
                ybuf[r, :, pl.ds(land, RADIUS)] = jnp.zeros(
                    (tile_x, RADIUS, depth), jnp.float32
                )

    for there, land in ((gx > 0, 0), (gx < n_gx - 1, RADIUS + tile_x)):

        @pl.when(jnp.logical_not(there))
        def _(land=land):
            for r in range(ROUNDS):
                xbuf[r, pl.ds(land, RADIUS)] = jnp.zeros(
                    (RADIUS, tile_y, depth), jnp.float32
                )

    group = RADIUS
    z_taps = depth_matrix(depth)

    peers = jnp.int32(len(others))
    for there, _ in (y_prev, y_next, *x_sides):
        peers = peers + there.astype(jnp.int32)
    pl.semaphore_wait(barrier, peers)

    def y_copy(r, d, i, source=None):
        p, n = pieces[i]
        part = pl.ds(p, n)
        if d == 0:
            rows, land, device = RADIUS, RADIUS + tile_y, y_prev[1]
        else:
            rows, land, device = tile_y, 0, y_next[1]
        if source is None:
            src = ybuf.at[r, part, pl.ds(rows, RADIUS)]
        else:
            src = source.at[part, pl.ds(rows - RADIUS, RADIUS)]
        return pltpu.make_async_remote_copy(
            src_ref=src,
            dst_ref=ybuf.at[r, part, pl.ds(land, RADIUS)],
            send_sem=y_send.at[r, d, i],
            recv_sem=y_recv.at[r, d, i],
            device_id=device,
            device_id_type=MESH,
        )

    def x_copy(r, i, back=False):
        start = pieces[i][0]
        high = side if i == 0 else 1 - side
        if back:
            land = high * (tile_x + RADIUS)
        else:
            land = (1 - high) * (tile_x + RADIUS)
        sent, got = (1 - high, high)
        return pltpu.make_async_remote_copy(
            src_ref=xbuf.at[r, pl.ds(RADIUS + start, RADIUS)],
            dst_ref=xbuf.at[r, pl.ds(land, RADIUS)],
            send_sem=x_send.at[r, i],
            recv_sem=x_recv.at[r, got if back else sent],
            device_id=x_sides[i][1],
            device_id_type=MESH,
        )

    def s_copy(k, i):
        part = pl.ds(*pieces[i])
        return pltpu.make_async_remote_copy(
            src_ref=sens.at[me, part],
            dst_ref=sens.at[me, part],
            send_sem=s_send.at[k, i],
            recv_sem=s_recv.at[k, i],
            device_id=others[k],
            device_id_type=MESH,
        )

    def y_start(r, i, source=None):
        for d, (there, _) in enumerate((y_prev, y_next)):

            @pl.when(there)
            def _(d=d):
                y_copy(r, d, i, source).start()

    def y_arrive(r, i):
        for d, (there, _) in enumerate((y_next, y_prev)):

            @pl.when(there)
            def _(d=d):
                y_copy(r, d, i).wait_recv()

    for i in range(len(pieces)):
        y_start(0, i, den)

    for i, (p, n) in enumerate(pieces):
        loads["f", i].wait()
        loads["a", i].wait()
        for q in [p + j for j in range(n)]:
            total = None
            for s in range(sources):
                real, imag = None, None
                for c in range(comps):
                    a = fbuf[s, 0, c, q].astype(jnp.float32) * abuf[s, 0, c, q].astype(
                        jnp.float32
                    )
                    b = fbuf[s, 1, c, q].astype(jnp.float32) * abuf[s, 1, c, q].astype(
                        jnp.float32
                    )
                    real = (a - b) if real is None else real + (a - b)
                term = weight[s] * real
                total = term if total is None else total + term
            sens[me, q] = total
        for k in range(len(others)):
            s_copy(k, i).start()

    def y_filter(r, i):
        p, n = pieces[i]
        for g in [p + j for j in range(0, n, group)]:
            total = None
            for k in range(RADIUS + 1):
                row = ybuf[r, pl.ds(g, group), pl.ds(k, tile_y)]
                if k < RADIUS:
                    row = row + ybuf[
                        r, pl.ds(g, group), pl.ds(2 * RADIUS - k, tile_y)
                    ]
                row = row * float(k + 1)
                total = row if total is None else total + row
            xbuf[r, pl.ds(RADIUS + g, group)] = total

    def xz_filter(r, i):
        p, n = pieces[i]
        halves = []
        for h in range(0, tile_y, 8):
            value = xbuf[r, pl.ds(p, n + 2 * RADIUS), pl.ds(h, 8)]
            halves.append(box(box(value)))
        value = jnp.concatenate(halves, axis=1).reshape(n * tile_y, depth)
        both = jnp.concatenate(split(value), axis=1)
        out = jnp.dot(both, z_taps, preferred_element_type=jnp.float32)
        return (out * NORM).reshape(n, tile_y, depth)

    def through_x(r):
        for i in (0, 1):
            y_arrive(r, i)
            y_filter(r, i)
            there = x_sides[i][0]

            @pl.when(there)
            def _(i=i):
                x_copy(r, i).start()

        y_arrive(r, 2)
        y_filter(r, 2)

    def x_arrive(r, i):
        there = x_sides[i][0]

        @pl.when(there)
        def _():
            x_copy(r, i, back=True).wait_recv()

    def chain(i, filtered):
        p, n = pieces[i]
        part = pl.ds(p, n)
        for k in range(len(others)):
            source = lax.rem(me + n_illum - 1 - k, n_illum)
            pltpu.make_async_remote_copy(
                src_ref=sens.at[me, part],
                dst_ref=sens.at[source, part],
                send_sem=s_send.at[k, i],
                recv_sem=s_recv.at[k, i],
                device_id=others[k],
                device_id_type=MESH,
            ).wait_recv()
        total = sens[0, part]
        for e in range(1, n_illum):
            total = total + sens[e, part]
        inner = jnp.tanh(SHARPNESS * (filtered - THRESHOLD))
        ybuf[1, part, own] = total * (
            SHARPNESS * (1.0 - inner * inner) * (1.0 / SCALE)
        )
        y_start(1, i)

    def update(i, gradient):
        part = pl.ds(*pieces[i])
        one = 0.9 * m1buf[part] + 0.1 * gradient
        two = 0.999 * m2buf[part] + 0.001 * gradient * gradient
        new_m1[part] = one
        new_m2[part] = two
        step = one * FIRST_FIX / (jnp.sqrt(two * SECOND_FIX) + 1e-08)
        value = jnp.clip(ybuf[0, part, own] - 0.05 * step, 0.0, 1.0)
        ybuf[2, part, own] = value
        y_start(2, i)
        new_den[part] = value

    def finish(i, value):
        part = pl.ds(*pieces[i])
        physical[part] = (TANH_EDGE + jnp.tanh(SHARPNESS * (value - THRESHOLD))) * (
            1.0 / SCALE
        )

    loads["d"].wait()
    through_x(0)
    filt[...] = xz_filter(0, 2)
    for i in (0, 1):
        x_arrive(0, i)
        chain(i, xz_filter(0, i))
    chain(2, filt[...])

    loads["m1"].wait()
    loads["m2"].wait()
    through_x(1)
    filt[...] = xz_filter(1, 2)
    for i in (0, 1):
        x_arrive(1, i)
        update(i, xz_filter(1, i))
    update(2, filt[...])
    through_x(2)
    finish(2, xz_filter(2, 2))
    for i in (0, 1):
        x_arrive(2, i)
        finish(i, xz_filter(2, i))

    for i in range(len(pieces)):
        for k in range(len(others)):
            s_copy(k, i).wait_send()
    for d in (0, 1):

        @pl.when((y_prev, y_next)[d][0])
        def _(d=d):
            for r in range(ROUNDS):
                for i in range(len(pieces)):
                    y_copy(r, d, i, den if r == 0 else None).wait_send()

        @pl.when(x_sides[d][0])
        def _(d=d):
            for r in range(ROUNDS):
                x_copy(r, d).wait_send()


def export(a, b, c, d, a_out, b_out, c_out, d_out, sem):
    copies = [
        pltpu.make_async_copy(src, dst, sem.at[i])
        for i, (src, dst) in enumerate(
            ((a, a_out), (b, b_out), (c, c_out), (d, d_out))
        )
    ]
    for copy in copies:
        copy.start()
    for copy in copies:
        copy.wait()


def shards(sizes, density, moment_one, moment_two, forward_field, adjoint_field, objective_weight):
    tile_x, tile_y, depth = density.shape
    n_illum = sizes[0]
    tile = jax.ShapeDtypeStruct(density.shape, jnp.float32)
    f32 = jnp.float32
    far = max(n_illum - 1, 1)
    arguments = [
        pltpu.with_memory_space_constraint(x, pltpu.HBM)
        for x in (density, moment_one, moment_two, forward_field, adjoint_field)
    ]
    results = pl.pallas_call(
        functools.partial(kernel, sizes),
        out_shape=(pltpu.VMEM(density.shape, f32),) * 4,
        in_specs=[pl.BlockSpec(memory_space=pltpu.HBM)] * 5
        + [pl.BlockSpec(memory_space=pltpu.SMEM)],
        out_specs=(pl.BlockSpec(memory_space=pltpu.VMEM),) * 4,
        scratch_shapes=[
            pltpu.VMEM((ROUNDS, tile_x, tile_y + 2 * RADIUS, depth), f32),
            pltpu.VMEM((ROUNDS, tile_x + 2 * RADIUS, tile_y, depth), f32),
            pltpu.VMEM((n_illum, tile_x, tile_y, depth), f32),
            pltpu.VMEM(forward_field.shape, forward_field.dtype),
            pltpu.VMEM(adjoint_field.shape, adjoint_field.dtype),
            pltpu.VMEM(density.shape, f32),
            pltpu.VMEM(density.shape, f32),
            pltpu.VMEM((tile_x - 2 * RADIUS, tile_y, depth), f32),
            pltpu.SemaphoreType.DMA((9,)),
            pltpu.SemaphoreType.DMA((ROUNDS, 2, 3)),
            pltpu.SemaphoreType.DMA((ROUNDS, 2, 3)),
            pltpu.SemaphoreType.DMA((ROUNDS, 2)),
            pltpu.SemaphoreType.DMA((ROUNDS, 2)),
            pltpu.SemaphoreType.DMA((far, 3)),
            pltpu.SemaphoreType.DMA((far, 3)),
        ],
        compiler_params=pltpu.CompilerParams(
            collective_id=0, has_side_effects=True, vmem_limit_bytes=48 << 20
        ),
        name="design_update",
    )(*arguments, objective_weight)
    return pl.pallas_call(
        export,
        out_shape=(tile,) * 4,
        in_specs=[pl.BlockSpec(memory_space=pltpu.VMEM)] * 4,
        out_specs=(pl.BlockSpec(memory_space=pl.ANY),) * 4,
        scratch_shapes=[pltpu.SemaphoreType.DMA((4,))],
        compiler_params=pltpu.CompilerParams(vmem_limit_bytes=4 << 20),
        name="export_results",
    )(*results)


def solution(mesh):
    field = P("illum", None, None, "gx", "gy", None)
    tile = P("gx", "gy", None)
    sizes = (mesh.shape["illum"], mesh.shape["gx"], mesh.shape["gy"])
    return jax.shard_map(
        functools.partial(shards, sizes),
        mesh=mesh,
        in_specs=(tile, tile, tile, field, field, P("illum")),
        out_specs=(tile,) * 4,
        check_vma=False,
    )
```

```python
import functools
import math

import jax
import jax.numpy as jnp
from jax import lax
from jax.experimental import pallas as pl
from jax.experimental.pallas import tpu as pltpu
from jax.sharding import PartitionSpec as P

RADIUS = 8
SHARPNESS = 8.0
THRESHOLD = 0.5
TANH_EDGE = math.tanh(SHARPNESS * THRESHOLD)
SCALE = math.tanh(SHARPNESS * THRESHOLD) + math.tanh(SHARPNESS * (1.0 - THRESHOLD))
NORM = 1.0 / float((RADIUS + 1) ** 6)
FIRST_FIX = 1.0 / (1.0 - 0.9**5)
SECOND_FIX = 1.0 / (1.0 - 0.999**5)
MESH = pl.DeviceIdType.MESH
ROUNDS = 3


def split(value):
    high = value.astype(jnp.bfloat16)
    low = (value - high.astype(jnp.float32)).astype(jnp.bfloat16)
    return high, low


def box(value):
    n = value.shape[0]
    two = value[: n - 1] + value[1:]
    four = two[: n - 3] + two[2:]
    eight = four[: n - 7] + four[4:]
    return eight[: n - 8] + value[8:]


def depth_matrix(length):
    row = lax.broadcasted_iota(jnp.int32, (2 * length, length), 0)
    col = lax.broadcasted_iota(jnp.int32, (2 * length, length), 1)
    row = jnp.where(row >= length, row - length, row)
    taps = jnp.maximum(RADIUS + 1 - jnp.abs(row - col), 0)
    return taps.astype(jnp.float32).astype(jnp.bfloat16)


def kernel(
    sizes,
    den,
    m1,
    m2,
    fwd,
    adj,
    weight,
    new_den,
    new_m1,
    new_m2,
    physical,
    ybuf,
    xbuf,
    sens,
    fbuf,
    abuf,
    m1buf,
    m2buf,
    filt,
    local_sem,
    y_send,
    y_recv,
    x_send,
    x_recv,
    s_send,
    s_recv,
):
    n_illum, n_gx, n_gy = sizes
    tile_x, tile_y, depth = den.shape
    sources, _, comps = fwd.shape[:3]
    me = lax.axis_index("illum")
    gx = lax.axis_index("gx")
    gy = lax.axis_index("gy")
    side = (gx < n_gx // 2).astype(jnp.int32)
    reach = tile_x - RADIUS
    pieces = [
        (side * reach, RADIUS),
        ((1 - side) * reach, RADIUS),
        (RADIUS, tile_x - 2 * RADIUS),
    ]
    own = pl.ds(RADIUS, tile_y)

    loads = {}

    def load(name, src, dst):
        copy = pltpu.make_async_copy(src, dst, local_sem.at[len(loads)])
        copy.start()
        loads[name] = copy

    for i, (p, n) in enumerate(pieces):
        part = pl.ds(p, n)
        load(("f", i), fwd.at[:, :, :, part], fbuf.at[:, :, :, part])
        load(("a", i), adj.at[:, :, :, part], abuf.at[:, :, :, part])
    load("d", den, ybuf.at[0, :, own])
    load("m1", m1, m1buf)
    load("m2", m2, m2buf)

    near, far = gx + 2 * side - 1, gx - 2 * side + 1
    x_sides = [
        (jnp.logical_and(at >= 0, at < n_gx), {"gx": jnp.clip(at, 0, n_gx - 1)})
        for at in (near, far)
    ]
    y_prev = (gy > 0, {"gy": jnp.maximum(gy - 1, 0)})
    y_next = (gy < n_gy - 1, {"gy": jnp.minimum(gy + 1, n_gy - 1)})
    others = [{"illum": lax.rem(me + k, n_illum)} for k in range(1, n_illum)]

    barrier = pltpu.get_barrier_semaphore()
    for there, device in (y_prev, y_next, *x_sides):

        @pl.when(there)
        def _(device=device):
            pl.semaphore_signal(barrier, inc=1, device_id=device, device_id_type=MESH)

    for device in others:
        pl.semaphore_signal(barrier, inc=1, device_id=device, device_id_type=MESH)
    for there, land in ((y_prev[0], 0), (y_next[0], RADIUS + tile_y)):

        @pl.when(jnp.logical_not(there))
        def _(land=land):
            for r in range(ROUNDS):
                ybuf[r, :, pl.ds(land, RADIUS)] = jnp.zeros(
                    (tile_x, RADIUS, depth), jnp.float32
                )

    for there, land in ((gx > 0, 0), (gx < n_gx - 1, RADIUS + tile_x)):

        @pl.when(jnp.logical_not(there))
        def _(land=land):
            for r in range(ROUNDS):
                xbuf[r, pl.ds(land, RADIUS)] = jnp.zeros(
                    (RADIUS, tile_y, depth), jnp.float32
                )

    group = RADIUS
    z_taps = depth_matrix(depth)

    peers = jnp.int32(len(others))
    for there, _ in (y_prev, y_next, *x_sides):
        peers = peers + there.astype(jnp.int32)
    pl.semaphore_wait(barrier, peers)

    def y_copy(r, d, i, source=None):
        p, n = pieces[i]
        part = pl.ds(p, n)
        if d == 0:
            rows, land, device = RADIUS, RADIUS + tile_y, y_prev[1]
        else:
            rows, land, device = tile_y, 0, y_next[1]
        if source is None:
            src = ybuf.at[r, part, pl.ds(rows, RADIUS)]
        else:
            src = source.at[part, pl.ds(rows - RADIUS, RADIUS)]
        return pltpu.make_async_remote_copy(
            src_ref=src,
            dst_ref=ybuf.at[r, part, pl.ds(land, RADIUS)],
            send_sem=y_send.at[r, d, i],
            recv_sem=y_recv.at[r, d, i],
            device_id=device,
            device_id_type=MESH,
        )

    def x_copy(r, i, back=False):
        start = pieces[i][0]
        high = side if i == 0 else 1 - side
        if back:
            land = high * (tile_x + RADIUS)
        else:
            land = (1 - high) * (tile_x + RADIUS)
        sent, got = (1 - high, high)
        return pltpu.make_async_remote_copy(
            src_ref=xbuf.at[r, pl.ds(RADIUS + start, RADIUS)],
            dst_ref=xbuf.at[r, pl.ds(land, RADIUS)],
            send_sem=x_send.at[r, i],
            recv_sem=x_recv.at[r, got if back else sent],
            device_id=x_sides[i][1],
            device_id_type=MESH,
        )

    def s_copy(k, i):
        part = pl.ds(*pieces[i])
        return pltpu.make_async_remote_copy(
            src_ref=sens.at[me, part],
            dst_ref=sens.at[me, part],
            send_sem=s_send.at[k, i],
            recv_sem=s_recv.at[k, i],
            device_id=others[k],
            device_id_type=MESH,
        )

    def y_start(r, i, source=None):
        for d, (there, _) in enumerate((y_prev, y_next)):

            @pl.when(there)
            def _(d=d):
                y_copy(r, d, i, source).start()

    def y_arrive(r, i):
        for d, (there, _) in enumerate((y_next, y_prev)):

            @pl.when(there)
            def _(d=d):
                y_copy(r, d, i).wait_recv()

    for i in range(len(pieces)):
        y_start(0, i, den)

    for i, (p, n) in enumerate(pieces):
        loads["f", i].wait()
        loads["a", i].wait()
        for q in [p + j for j in range(n)]:
            total = None
            for s in range(sources):
                real, imag = None, None
                for c in range(comps):
                    a = fbuf[s, 0, c, q].astype(jnp.float32) * abuf[s, 0, c, q].astype(
                        jnp.float32
                    )
                    b = fbuf[s, 1, c, q].astype(jnp.float32) * abuf[s, 1, c, q].astype(
                        jnp.float32
                    )
                    real = (a - b) if real is None else real + (a - b)
                term = weight[s] * real
                total = term if total is None else total + term
            sens[me, q] = total
        for k in range(len(others)):
            s_copy(k, i).start()

    def y_filter(r, i):
        p, n = pieces[i]
        for g in [p + j for j in range(0, n, group)]:
            total = None
            for k in range(RADIUS + 1):
                row = ybuf[r, pl.ds(g, group), pl.ds(k, tile_y)]
                if k < RADIUS:
                    row = row + ybuf[
                        r, pl.ds(g, group), pl.ds(2 * RADIUS - k, tile_y)
                    ]
                row = row * float(k + 1)
                total = row if total is None else total + row
            xbuf[r, pl.ds(RADIUS + g, group)] = total

    def xz_filter(r, i):
        p, n = pieces[i]
        halves = []
        for h in range(0, tile_y, 8):
            value = xbuf[r, pl.ds(p, n + 2 * RADIUS), pl.ds(h, 8)]
            halves.append(box(box(value)))
        value = jnp.concatenate(halves, axis=1).reshape(n * tile_y, depth)
        both = jnp.concatenate(split(value), axis=1)
        out = jnp.dot(both, z_taps, preferred_element_type=jnp.float32)
        return (out * NORM).reshape(n, tile_y, depth)

    def through_x(r):
        for i in (0, 1):
            y_arrive(r, i)
            y_filter(r, i)
            there = x_sides[i][0]

            @pl.when(there)
            def _(i=i):
                x_copy(r, i).start()

        y_arrive(r, 2)
        y_filter(r, 2)

    def x_arrive(r, i):
        there = x_sides[i][0]

        @pl.when(there)
        def _():
            x_copy(r, i, back=True).wait_recv()

    def chain(i, filtered):
        p, n = pieces[i]
        part = pl.ds(p, n)
        for k in range(len(others)):
            source = lax.rem(me + n_illum - 1 - k, n_illum)
            pltpu.make_async_remote_copy(
                src_ref=sens.at[me, part],
                dst_ref=sens.at[source, part],
                send_sem=s_send.at[k, i],
                recv_sem=s_recv.at[k, i],
                device_id=others[k],
                device_id_type=MESH,
            ).wait_recv()
        total = sens[0, part]
        for e in range(1, n_illum):
            total = total + sens[e, part]
        inner = jnp.tanh(SHARPNESS * (filtered - THRESHOLD))
        ybuf[1, part, own] = total * (
            SHARPNESS * (1.0 - inner * inner) * (1.0 / SCALE)
        )
        y_start(1, i)

    def update(i, gradient):
        part = pl.ds(*pieces[i])
        one = 0.9 * m1buf[part] + 0.1 * gradient
        two = 0.999 * m2buf[part] + 0.001 * gradient * gradient
        new_m1[part] = one
        new_m2[part] = two
        step = one * FIRST_FIX / (jnp.sqrt(two * SECOND_FIX) + 1e-08)
        value = jnp.clip(ybuf[0, part, own] - 0.05 * step, 0.0, 1.0)
        ybuf[2, part, own] = value
        y_start(2, i)
        new_den[part] = value

    def finish(i, value):
        part = pl.ds(*pieces[i])
        physical[part] = (TANH_EDGE + jnp.tanh(SHARPNESS * (value - THRESHOLD))) * (
            1.0 / SCALE
        )

    loads["d"].wait()
    through_x(0)
    filt[...] = xz_filter(0, 2)
    for i in (0, 1):
        x_arrive(0, i)
        chain(i, xz_filter(0, i))
    chain(2, filt[...])

    loads["m1"].wait()
    loads["m2"].wait()
    through_x(1)
    filt[...] = xz_filter(1, 2)
    for i in (0, 1):
        x_arrive(1, i)
        update(i, xz_filter(1, i))
    update(2, filt[...])
    through_x(2)
    finish(2, xz_filter(2, 2))
    for i in (1, 0):
        x_arrive(2, i)
        finish(i, xz_filter(2, i))

    for i in range(len(pieces)):
        for k in range(len(others)):
            s_copy(k, i).wait_send()
    for d in (0, 1):

        @pl.when((y_prev, y_next)[d][0])
        def _(d=d):
            for r in range(ROUNDS):
                for i in range(len(pieces)):
                    y_copy(r, d, i, den if r == 0 else None).wait_send()

        @pl.when(x_sides[d][0])
        def _(d=d):
            for r in range(ROUNDS):
                x_copy(r, d).wait_send()


def export(a, b, c, d, a_out, b_out, c_out, d_out, sem):
    copies = [
        pltpu.make_async_copy(src, dst, sem.at[i])
        for i, (src, dst) in enumerate(
            ((a, a_out), (b, b_out), (c, c_out), (d, d_out))
        )
    ]
    for copy in copies:
        copy.start()
    for copy in copies:
        copy.wait()


def shards(sizes, density, moment_one, moment_two, forward_field, adjoint_field, objective_weight):
    tile_x, tile_y, depth = density.shape
    n_illum = sizes[0]
    tile = jax.ShapeDtypeStruct(density.shape, jnp.float32)
    f32 = jnp.float32
    far = max(n_illum - 1, 1)
    arguments = [
        pltpu.with_memory_space_constraint(x, pltpu.HBM)
        for x in (density, moment_one, moment_two, forward_field, adjoint_field)
    ]
    results = pl.pallas_call(
        functools.partial(kernel, sizes),
        out_shape=(pltpu.VMEM(density.shape, f32),) * 4,
        in_specs=[pl.BlockSpec(memory_space=pltpu.HBM)] * 5
        + [pl.BlockSpec(memory_space=pltpu.SMEM)],
        out_specs=(pl.BlockSpec(memory_space=pltpu.VMEM),) * 4,
        scratch_shapes=[
            pltpu.VMEM((ROUNDS, tile_x, tile_y + 2 * RADIUS, depth), f32),
            pltpu.VMEM((ROUNDS, tile_x + 2 * RADIUS, tile_y, depth), f32),
            pltpu.VMEM((n_illum, tile_x, tile_y, depth), f32),
            pltpu.VMEM(forward_field.shape, forward_field.dtype),
            pltpu.VMEM(adjoint_field.shape, adjoint_field.dtype),
            pltpu.VMEM(density.shape, f32),
            pltpu.VMEM(density.shape, f32),
            pltpu.VMEM((tile_x - 2 * RADIUS, tile_y, depth), f32),
            pltpu.SemaphoreType.DMA((9,)),
            pltpu.SemaphoreType.DMA((ROUNDS, 2, 3)),
            pltpu.SemaphoreType.DMA((ROUNDS, 2, 3)),
            pltpu.SemaphoreType.DMA((ROUNDS, 2)),
            pltpu.SemaphoreType.DMA((ROUNDS, 2)),
            pltpu.SemaphoreType.DMA((far, 3)),
            pltpu.SemaphoreType.DMA((far, 3)),
        ],
        compiler_params=pltpu.CompilerParams(
            collective_id=0, has_side_effects=True, vmem_limit_bytes=48 << 20
        ),
        name="design_update",
    )(*arguments, objective_weight)
    return pl.pallas_call(
        export,
        out_shape=(tile,) * 4,
        in_specs=[pl.BlockSpec(memory_space=pltpu.VMEM)] * 4,
        out_specs=(pl.BlockSpec(memory_space=pl.ANY),) * 4,
        scratch_shapes=[pltpu.SemaphoreType.DMA((4,))],
        compiler_params=pltpu.CompilerParams(vmem_limit_bytes=4 << 20),
        name="export_results",
    )(*results)


def solution(mesh):
    field = P("illum", None, None, "gx", "gy", None)
    tile = P("gx", "gy", None)
    sizes = (mesh.shape["illum"], mesh.shape["gx"], mesh.shape["gy"])
    return jax.shard_map(
        functools.partial(shards, sizes),
        mesh=mesh,
        in_specs=(tile, tile, tile, field, field, P("illum")),
        out_specs=(tile,) * 4,
        check_vma=False,
    )
```
